32 devices in a mesh: row: 4 (over z), col: 2 (over core), depth: 4 (over y, x).
Axes of the slice: x: 2, y: 2, z: 4, core: 2. Of those that a mesh axis runs over, the one named last changes fastest.
Arguments:
- lower_prev: float32 [3, 1024, 4096], P(None, 'row', 'depth'), may hold values from -0.09375 to 0.09375
- inner_blocks: float32 [3, 1024, 1024], P(None, 'row', 'depth'), may hold values from -0.1875 to 0.1875
- diag_inverse: float32 [3, 1024, 1024], P(None, 'depth'), as said below
- known_rows: float32 [4096, 2048], P('depth', 'col'), may hold values from -6 to 6
- right_sides: float32 [3, 1024, 2048], P(None, 'row', 'col'), may hold values from -6 to 6
Outputs:
- solved: float32 [3, 1024, 2048], P(None, 'depth', 'col')
The draws below stay inside these ranges and needn't reach their ends.
Inputs may be any that keep to these rules, and one draw needn't show every extreme that they name: Each diag_inverse[k] is lower triangular with diagonal entries between 0.7 and 1.3; its entries below the diagonal are of order 0.02 (normal with spread 0.6/4).
All inputs are finite; a program needn't handle non-finite values.
Results may differ from the reference program's by a relative error of at most 0.0001.
Values sent between devices are 32-bit elements; how exact they have to be, the bound alone decides.
No kernel may reach another device: no remote copies, remote signals or barrier semaphores. Data moves between devices by JAX's collectives and lax.ppermute only.
A program may use at most 64 MiB of HBM per device.

```python
import jax
import jax.numpy as jnp
from jax import lax

NB = 1024
RHS = 2048
PREV = 4096


def draw_diag_inverse(key, part):
    first_key = jax.random.fold_in(key, 11)
    second_key = jax.random.fold_in(key, 23)
    positions = jnp.arange(NB)
    below = positions[:, None] > positions[None, :]
    same = positions[:, None] == positions[None, :]
    off_diag = jax.random.normal(first_key, (3, NB, NB), jnp.float32) * (0.6 / NB ** 0.5)
    diagonal = jax.random.uniform(second_key, (3, NB, 1), jnp.float32, 0.7, 1.3)
    return jnp.where(below, off_diag, 0.0) + jnp.where(same, diagonal, 0.0)


def levels(own_key, extent, split, least, top_value):
    def one(axis_at, blocks):
        steps = jax.random.uniform(jax.random.fold_in(jax.random.fold_in(own_key, 6), axis_at), (blocks,), jnp.float32, least / len(split), top_value / len(split))
        return jnp.repeat(jnp.exp(steps), extent[axis_at] // blocks).reshape((-1,) + (1,) * (len(extent) - axis_at - 1))

    level = one(*split[0])
    for cut in split[1:]:
        level = level * one(*cut)
    return level


def normal_values(rng, extent, spread, most, pieces=(), dtype=jnp.bfloat16):
    loudness = levels(rng, extent, pieces, -0.22, 0.18) if pieces else 1.0
    result = jax.random.normal(rng, extent, jnp.float32) * spread * loudness
    return jnp.minimum(jnp.maximum(result, -most), most).astype(dtype)


def setup_inputs(seed: int = 0) -> dict:
    keys = jax.random.split(jax.random.key(seed), 6)
    lower_prev = normal_values(keys[0], (3, NB, PREV), PREV ** -0.5, 0.09375, ((1, 4), (2, 4)), jnp.float32)
    inner_blocks = normal_values(keys[1], (3, NB, NB), NB ** -0.5, 0.1875, ((1, 4), (2, 4)), jnp.float32)
    diag_inverse = draw_diag_inverse(jax.random.fold_in(keys[5], 71), 0)
    known_rows = normal_values(keys[3], (PREV, RHS), 1.0, 6.0, ((0, 4), (1, 2)), jnp.float32)
    right_sides = normal_values(keys[4], (3, NB, RHS), 1.0, 6.0, ((1, 4), (2, 2)), jnp.float32)
    return {"lower_prev": lower_prev, "inner_blocks": inner_blocks, "diag_inverse": diag_inverse, "known_rows": known_rows, "right_sides": right_sides}


def reference(lower_prev, inner_blocks, diag_inverse, known_rows, right_sides):
    highest = lax.Precision.HIGHEST
    earlier_map = [[], [(0, 0)], [(0, 1), (1, 2)]]
    solved = []
    for section in range(3):
        update = jnp.dot(lower_prev[section], known_rows, precision=highest, preferred_element_type=jnp.float32)
        for earlier, which in earlier_map[section]:
            update = update + jnp.dot(inner_blocks[which], solved[earlier], precision=highest, preferred_element_type=jnp.float32)
        reduced = right_sides[section] - update
        solved.append(jnp.dot(diag_inverse[section], reduced, precision=highest, preferred_element_type=jnp.float32))
    return jnp.stack(solved)
```

```python
import jax
import jax.numpy as jnp
from jax import lax
from jax.sharding import PartitionSpec as P


def dot(a, b):
    return jnp.dot(a, b, precision=lax.Precision.HIGH, preferred_element_type=jnp.float32)


def pick(array, axis, which, size):
    return lax.dynamic_slice_in_dim(array, which * size, size, axis)


def gather_row(piece, count):
    upward = [(j, j + 1) for j in range(count - 1)]
    downward = [(j + 1, j) for j in range(count - 1)]
    if count > 4:
        index = lax.axis_index("row")
        whole = lax.all_gather(piece, "row")
        return [lax.dynamic_index_in_dim(whole, (index - i) % count, 0, False) for i in range(count)]
    up, down = [piece], [piece]
    for _ in range(count - 1):
        up.append(lax.ppermute(up[-1], "row", upward))
        down.append(lax.ppermute(down[-1], "row", downward))
    index = lax.axis_index("row")
    return [piece] + [jnp.where(index >= i, up[i], down[count - i]) for i in range(1, count)]


def make(mesh):
    rows_n = mesh.shape["row"]
    depth_n = mesh.shape["depth"]
    swap_x = [(d, d ^ 1) for d in range(depth_n)]
    swap_y = [(d, d ^ 2) for d in range(depth_n)]
    swap_core = [(0, 1), (1, 0)]

    def on_device(lower_prev, inner_blocks, diag_inverse, known_rows, right_sides):
        z = lax.axis_index("row")
        d = lax.axis_index("depth")
        core = lax.axis_index("col")
        x, y = d % 2, d // 2
        rl = lower_prev.shape[1]
        h = rl // 2
        cols = known_rows.shape[1]
        half = cols // 2
        w = half // rows_n
        nb = rl * rows_n

        dh = diag_inverse.shape[1] // 2
        d_mine = pick(diag_inverse, 1, core, dh)
        d_rest = pick(diag_inverse, 1, 1 - core, dh)
        lw = inner_blocks.shape[2] // 2
        l_mine = pick(inner_blocks, 2, core, lw)

        def diag_pair(k):
            near = lax.ppermute(d_mine[k], "depth", swap_x)
            far = lax.ppermute(near, "col", swap_core)
            return jnp.concatenate([d_mine[k], near, d_rest[k], far], 0)

        def inner_pair(lo, hi):
            mine = l_mine[lo:hi]
            near = lax.ppermute(mine, "depth", swap_x)
            joined = jnp.concatenate([mine, near], 2)
            pieces = gather_row(joined, rows_n)
            full = jnp.zeros((rows_n,) + joined.shape, joined.dtype)
            for i, piece in enumerate(pieces):
                full = lax.dynamic_update_index_in_dim(full, piece, (z - i) % rows_n, 0)
            other = lax.ppermute(full, "col", swap_core)
            both = jnp.concatenate([full, other], 3)
            return [both[:, i].reshape(nb, 4 * lw) for i in range(hi - lo)]

        diag0 = diag_pair(0)
        inner10 = inner_pair(0, 1)[0]

        def rhs_block(k):
            return pick(pick(right_sides[k], 0, y, h), 1, x, half)

        part = dot(lower_prev[0], known_rows)
        p5 = part.reshape(rl, 2, 2, half // 2)
        a, b = p5[:, :, 0], p5[:, :, 1]
        a_got = lax.ppermute(pick(a, 1, 1 - x, 1)[:, 0], "depth", swap_x)
        b_got = lax.ppermute(pick(b, 0, 1 - y, h), "depth", swap_y)
        a = pick(a, 1, x, 1)[:, 0] + a_got
        b = pick(b, 0, y, h) + b_got
        a_got = lax.ppermute(pick(a, 0, 1 - y, h), "depth", swap_y)
        b_got = lax.ppermute(pick(b, 1, 1 - x, 1)[:, 0], "depth", swap_x)
        a = pick(a, 0, y, h) + a_got
        b = pick(b, 1, x, 1)[:, 0] + b_got
        first = rhs_block(0) - jnp.concatenate([a, b], 1)

        def spread(block):
            v = block.reshape(h, rows_n, w).transpose(1, 0, 2)
            return lax.all_to_all(v, "row", 0, 0, tiled=True)

        own = spread(first)

        p1 = dot(lower_prev[1], known_rows)
        p2 = dot(lower_prev[2], known_rows)
        g1 = lax.ppermute(pick(p1, 1, 1 - x, half), "depth", swap_x)
        g2 = lax.ppermute(pick(p2, 0, 1 - y, h), "depth", swap_y)
        p1 = pick(p1, 1, x, half) + g1
        p2 = pick(p2, 0, y, h) + g2
        g1 = lax.ppermute(pick(p1, 0, 1 - y, h), "depth", swap_y)
        g2 = lax.ppermute(pick(p2, 1, 1 - x, half), "depth", swap_x)
        p1 = rhs_block(1) - (pick(p1, 0, y, h) + g1)
        p2 = rhs_block(2) - (pick(p2, 1, x, half) + g2)
        v = jnp.stack([p1, p2]).reshape(2, h, rows_n, w).transpose(2, 0, 1, 3)
        later = lax.all_to_all(v, "row", 0, 0, tiled=True)
        waiting = [None, later[:, 0], later[:, 1]]

        diag1 = diag_pair(1)
        inner20, inner21 = inner_pair(1, 3)
        diag2 = diag_pair(2)
        diags = [diag0, diag1, diag2]

        outs = []
        carried = None
        for k in range(3):
            got = lax.ppermute(own, "depth", swap_y)
            reduced = jnp.stack([jnp.where(y == 0, own, got), jnp.where(y == 0, got, own)], 1)
            reduced = reduced.reshape(nb, w)
            value = dot(diags[k], reduced)
            if k == 0:
                update = dot(inner10, value)
                carried = dot(inner20, value)
            elif k == 1:
                update = carried + dot(inner21, value)
            if k < 2:
                u = update.reshape(rows_n, 2, h, w)
                got = lax.ppermute(pick(u, 1, 1 - y, 1)[:, 0], "depth", swap_y)
                own = waiting[k + 1] - (pick(u, 1, y, 1)[:, 0] + got)
            v4 = value.reshape(2, 2, dh, w)
            swapped = lax.ppermute(v4[:, 1], "depth", swap_x)
            pieces = gather_row(jnp.stack([v4[:, 0], swapped]), rows_n)
            full = jnp.zeros((rows_n,) + pieces[0].shape, jnp.float32)
            for i, piece in enumerate(pieces):
                full = lax.dynamic_update_index_in_dim(full, piece, (z - i) % rows_n, 0)
            full = jnp.where(x == 0, full, full[:, ::-1])
            full = jnp.where(core == 0, full, full[:, :, ::-1])
            outs.append(full.transpose(2, 3, 1, 0, 4).reshape(2 * dh, cols))
        return jnp.stack(outs)

    return on_device


def solution(mesh):
    placed = (
        P(None, "row", "depth"),
        P(None, "row", "depth"),
        P(None, "depth", None),
        P("depth", "col"),
        P(None, "row", "col"),
    )
    return jax.shard_map(
        make(mesh), mesh=mesh, in_specs=placed, out_specs=P(None, "depth", "col"), check_vma=False
    )
```

```python
import functools

import jax
import jax.numpy as jnp
from jax import lax
from jax.experimental import pallas as pl
from jax.experimental.pallas import tpu as pltpu
from jax.sharding import PartitionSpec as P


F32 = jnp.float32
BF16 = jnp.bfloat16
SMEM = pl.BlockSpec(memory_space=pltpu.SMEM)
VMEM = pl.BlockSpec(memory_space=pltpu.VMEM)


def split(v):
    high = v.astype(BF16)
    return high, (v - high.astype(F32)).astype(BF16)


def mul(a, b):
    return jnp.dot(a, b, preferred_element_type=F32)


def mul3(a, b_high, b_both):
    a_high, a_low = split(a)
    n = b_high.shape[1]
    wide = mul(a_high, b_both)
    return wide[:, :n] + wide[:, n:] + mul(a_low, b_high)


def cost(flops, nbytes):
    return pl.CostEstimate(flops=flops, bytes_accessed=nbytes, transcendentals=0)


def gate(value, *before):
    return lax.optimization_barrier((value,) + before)[0]


def prev_kernel(h, w, a_ref, k_ref, o_ref):
    a_high, a_low = split(a_ref[...])
    k_high, k_low = split(k_ref[...])
    part = mul(a_high, k_high) + mul(a_high, k_low) + mul(a_low, k_high)
    for yy in range(2):
        for j in range(part.shape[1] // w):
            o_ref[yy, 0, j] = part[yy * h : (yy + 1) * h, j * w : (j + 1) * w]


def prev_product(lower_prev, known_rows, k, rows_n, h, w):
    rl, inner = lower_prev.shape[1:]
    cols = known_rows.shape[1]
    per = rows_n // 2
    return pl.pallas_call(
        functools.partial(prev_kernel, h, w),
        grid=(4,),
        in_specs=[
            pl.BlockSpec((None, rl, inner), lambda j: (k, 0, 0)),
            pl.BlockSpec((inner, per * w), lambda j: (0, j)),
        ],
        out_specs=pl.BlockSpec((2, 1, per, h, w), lambda j: (0, j // 2, j % 2, 0, 0)),
        out_shape=jax.ShapeDtypeStruct((2, 2, rows_n, h, w), F32),
        cost_estimate=cost(2 * rl * inner * cols * 3, 4 * (rl * inner + inner * cols + rl * cols)),
        name=f"prev{k}",
    )(lower_prev, known_rows)


def sum_kernel(w, s_ref, p_ref, b_ref, o_ref):
    for j in range(o_ref.shape[0]):
        total = (p_ref[0, j] + p_ref[1, j]) + (p_ref[2, j] + p_ref[3, j])
        o_ref[j] = b_ref[:, j * w : (j + 1) * w] - total


def sum_parts(place, parts, right_sides, k):
    depth_n, rows_n, h, w = parts.shape
    return pl.pallas_call(
        functools.partial(sum_kernel, w),
        grid_spec=pltpu.PrefetchScalarGridSpec(
            num_scalar_prefetch=1,
            grid=(1,),
            in_specs=[
                pl.BlockSpec((depth_n, rows_n, h, w), lambda i, s: (0, 0, 0, 0)),
                pl.BlockSpec((None, h, rows_n * w), lambda i, s: (k, s[1], s[0])),
            ],
            out_specs=pl.BlockSpec((rows_n, h, w), lambda i, s: (0, 0, 0)),
        ),
        out_shape=jax.ShapeDtypeStruct((rows_n, h, w), F32),
        cost_estimate=cost(5 * rows_n * h * w, 24 * rows_n * h * w),
        name=f"sum{k}",
    )(place, parts, right_sides)


def step_kernel(k, rows_n, h, w, dh, s_ref, *refs):
    refs = list(refs)
    y, z, core = s_ref[1], s_ref[2], s_ref[3]
    value_ref = refs.pop()
    both_ref = refs.pop()
    a_ref, b_ref = refs.pop(0), refs.pop(0)
    if k == 0:
        for i in range(rows_n):
            for at, src in ((y, a_ref), (1 - y, b_ref)):
                high, low = split(src[i])
                value_ref[i, at, :, :w] = high
                value_ref[i, at, :, w:] = low
    else:
        if k == 1:
            mine_ref, theirs_ref = refs.pop(0), refs.pop(0)
        for i in range(rows_n):
            for at in range(2):
                total = -(a_ref[i, at] + b_ref[i, at])
                if k == 1:
                    total = total + jnp.where(y == at, mine_ref[i], theirs_ref[i])
                high, low = split(total)
                value_ref[i, at, :, :w] = high
                value_ref[i, at, :, w:] = low
    reduced = value_ref[...].reshape(rows_n * 2 * h, 2 * w)
    d_ref, near_ref, far_ref = refs.pop(0), refs.pop(0), refs.pop(0)
    blocks = (
        d_ref[pl.ds(pl.multiple_of(core * dh, dh), dh), :],
        near_ref[...],
        d_ref[pl.ds(pl.multiple_of((1 - core) * dh, dh), dh), :],
        far_ref[...],
    )
    own_out, swap_out = (refs[-3], refs[-2]) if k < 2 else (refs[-2], refs[-1])
    for n, block in enumerate(blocks):
        value = mul3(block, reduced[:, :w], reduced)
        (own_out, swap_out)[n % 2][n // 2] = value
        if k < 2:
            high, low = split(value)
            both_ref[n * dh : (n + 1) * dh, :w] = high
            both_ref[n * dh : (n + 1) * dh, w:] = low
    if k == 2:
        return
    u_ref = refs[-1]
    if k == 0:
        pack_ref, other_ref = refs[0], refs[1]
        for i in range(rows_n):
            row = jnp.concatenate(
                [pack_ref[i, 0], pack_ref[i, 1], other_ref[i, 0], other_ref[i, 1]], 1
            )
            u = mul3(row, both_ref[:, :w], both_ref[...])
            at = lax.rem(z + rows_n - i, rows_n)
            u_ref[at, 0] = u[:h]
            u_ref[at, 1] = u[h:]
    else:
        old_ref, wait_ref = refs[0], refs[1]
        mine, near, rest, far = refs[2:6]
        for i in range(rows_n):
            at = lax.rem(z + rows_n - i, rows_n)
            row = jnp.concatenate([mine[i, 1], near[i, 1], rest[i, 1], far[i, 1]], 1)
            u = mul3(row, both_ref[:, :w], both_ref[...])
            for part in range(2):
                u_ref[at, part] = (
                    u[part * h : (part + 1) * h]
                    + old_ref[at, part]
                    - jnp.where(y == part, wait_ref[at], 0.0)
                )


def carry_kernel(rows_n, h, w, s_ref, own_ref, swap_ref, mine, near, rest, far, u_ref, both_ref):
    z = s_ref[2]
    dh = own_ref.shape[1]
    for n, block in enumerate((own_ref[0], swap_ref[0], own_ref[1], swap_ref[1])):
        high, low = split(block)
        both_ref[n * dh : (n + 1) * dh, :w] = high
        both_ref[n * dh : (n + 1) * dh, w:] = low
    for i in range(rows_n):
        at = lax.rem(z + rows_n - i, rows_n)
        row = jnp.concatenate([mine[i, 0], near[i, 0], rest[i, 0], far[i, 0]], 1)
        u = mul3(row, both_ref[:, :w], both_ref[...])
        u_ref[at, 0] = u[:h]
        u_ref[at, 1] = u[h:]


def run_step(k, place, rows_n, h, w, dh, ins, diag, near, far, near_at, weights):
    nb = rows_n * 2 * h
    out = [jax.ShapeDtypeStruct((2, dh, w), F32)] * 2
    if k < 2:
        out.append(jax.ShapeDtypeStruct((rows_n, 2, h, w), F32))
    whole = pl.BlockSpec((None,) + diag.shape[1:], lambda i: (k, 0, 0))
    part = pl.BlockSpec((None,) + near.shape[1:], lambda i: (near_at, 0, 0))
    return pl.pallas_call(
        functools.partial(step_kernel, k, rows_n, h, w, dh),
        grid=(1,),
        in_specs=[SMEM] + [VMEM] * len(ins) + [whole, part, part] + [VMEM] * len(weights),
        out_specs=[VMEM] * len(out),
        out_shape=out,
        scratch_shapes=[pltpu.VMEM((4 * dh, 2 * w), BF16), pltpu.VMEM((rows_n, 2, h, 2 * w), BF16)],
        cost_estimate=cost(12 * nb * 4 * dh * w, 8 * nb * 4 * dh),
        name=f"step{k}",
    )(place, *ins, diag, near, far, *weights)


def run_carry(place, rows_n, h, w, own, swap, mats):
    dh = own.shape[1]
    return pl.pallas_call(
        functools.partial(carry_kernel, rows_n, h, w),
        in_specs=[SMEM] + [VMEM] * 6,
        out_specs=VMEM,
        out_shape=jax.ShapeDtypeStruct((rows_n, 2, h, w), F32),
        scratch_shapes=[pltpu.VMEM((4 * dh, 2 * w), BF16)],
        cost_estimate=cost(6 * rows_n * 2 * h * 4 * dh * w, 4 * rows_n * 2 * h * 4 * dh),
        name="carry",
    )(place, own, swap, *mats)


def place_kernel(rows_n, w, dh, split_pairs, s_ref, *refs):
    x, z, core = s_ref[0], s_ref[2], s_ref[3]
    o_ref = refs[-1]
    pieces = [refs[:2]]
    for i in range(1, rows_n):
        pieces.append(refs[2 * i : 2 * i + 2] if split_pairs else refs[i + 1])
    for i in range(rows_n):
        member = lax.rem(z + rows_n - i, rows_n)
        for rel in range(2):
            side = x if rel == 0 else 1 - x
            col = pl.multiple_of((side * rows_n + member) * w, w)
            for s in range(2):
                half = core if s == 0 else 1 - core
                row = pl.multiple_of(half * dh, dh)
                o_ref[pl.ds(row, dh), pl.ds(col, w)] = pieces[i][rel][s]


def place_rows(k, place, rows_n, w, dh, cols, ins, target=None):
    split_pairs = len(ins) == 2 * rows_n
    specs = [SMEM] + [VMEM] * len(ins)
    alias = {}
    if target is not None:
        ins = [*ins, target]
        specs.append(pl.BlockSpec(memory_space=pl.ANY))
        alias = {len(ins): 0}
    return pl.pallas_call(
        functools.partial(place_kernel, rows_n, w, dh, split_pairs),
        grid=(1,),
        in_specs=specs,
        out_specs=pl.BlockSpec((None, 2 * dh, cols), lambda i: (k, 0, 0)),
        out_shape=jax.ShapeDtypeStruct((3, 2 * dh, cols), F32),
        input_output_aliases=alias,
        cost_estimate=cost(0, 16 * dh * cols),
        name=f"place{k}",
    )(place, *ins)


def make(mesh):
    rows_n = mesh.shape["row"]
    depth_n = mesh.shape["depth"]
    swap_x = [(d, d ^ 1) for d in range(depth_n)]
    swap_y = [(d, d ^ 2) for d in range(depth_n)]
    swap_core = [(0, 1), (1, 0)]
    shifts = [[(j, (j + i) % rows_n) for j in range(rows_n)] for i in range(1, rows_n)]

    def over_x(v):
        return lax.ppermute(v, "depth", swap_x)

    def over_y(v):
        return lax.ppermute(v, "depth", swap_y)

    def over_core(v):
        return lax.ppermute(v, "col", swap_core)

    def over_row(v):
        return [lax.ppermute(v, "row", s) for s in shifts]

    def on_device(lower_prev, inner_blocks, diag_inverse, known_rows, right_sides):
        z = lax.axis_index("row")
        d = lax.axis_index("depth")
        core = lax.axis_index("col")
        place = jnp.stack([d % 2, d // 2, z, core]).astype(jnp.int32)
        h = lower_prev.shape[1] // 2
        cols = known_rows.shape[1]
        w = cols // (2 * rows_n)
        dh = diag_inverse.shape[1] // 2
        lw = inner_blocks.shape[2] // 2

        d_mine = lax.dynamic_slice_in_dim(diag_inverse, core * dh, dh, 1)
        l_mine = lax.dynamic_slice_in_dim(inner_blocks, core * lw, lw, 2)

        near10 = over_x(l_mine[0])
        part0 = prev_product(lower_prev, known_rows, 0, rows_n, h, w)
        got0 = lax.all_to_all(part0.reshape(depth_n, rows_n, h, w), "depth", 0, 0, tiled=True)
        pair10 = gate(jnp.stack([l_mine[0], near10]), part0)
        pack10 = jnp.stack([pair10] + over_row(pair10))
        other10 = over_core(pack10)

        part1 = prev_product(lower_prev, gate(known_rows, part0), 1, rows_n, h, w)
        sum0 = sum_parts(place, got0, right_sides, 0)
        own0 = lax.all_to_all(sum0, "row", 0, 0, tiled=True)

        d_first = gate(d_mine[:1], got0)
        near_d0 = over_x(d_first)
        far_d0 = over_core(near_d0)

        got1 = lax.all_to_all(part1.reshape(depth_n, rows_n, h, w), "depth", 0, 0, tiled=True)
        part2 = prev_product(lower_prev, gate(known_rows, part1), 2, rows_n, h, w)
        their0 = over_y(own0)

        later = gate(l_mine[1:], own0)
        pack2 = jnp.stack([later] + over_row(later))
        near2 = over_x(pack2)
        rest2 = over_core(pack2)
        far2 = over_core(near2)

        own_v0, swap_v0, u0 = run_step(
            0, place, rows_n, h, w, dh, [own0, their0], diag_inverse, near_d0, far_d0, 0, [pack10, other10]
        )
        v0 = over_y(u0)

        sum1 = sum_parts(place, got1, right_sides, 1)
        own1 = lax.all_to_all(sum1, "row", 0, 0, tiled=True)
        their1 = over_y(own1)
        got2 = lax.all_to_all(part2.reshape(depth_n, rows_n, h, w), "depth", 0, 0, tiled=True)
        sum2 = sum_parts(place, got2, right_sides, 2)
        own2 = lax.all_to_all(sum2, "row", 0, 0, tiled=True)

        near_d = over_x(gate(d_mine[1:], near2))
        far_d = over_core(near_d)

        swapped0 = over_x(swap_v0)
        carried = run_carry(place, rows_n, h, w, own_v0, swap_v0, (pack2, near2, rest2, far2))
        shifted0 = over_row(jnp.stack([own_v0, swapped0]))

        own_v1, swap_v1, u1 = run_step(
            1, place, rows_n, h, w, dh, [u0, v0, own1, their1], diag_inverse, near_d, far_d, 0,
            [carried, own2, pack2, near2, rest2, far2],
        )
        v1 = over_y(u1)
        swapped1 = over_x(swap_v1)
        shifted1 = over_row(jnp.stack([own_v1, swapped1]))

        own_v2, swap_v2 = run_step(
            2, place, rows_n, h, w, dh, [u1, v1], diag_inverse, near_d, far_d, 1, []
        )
        own_shift = over_row(own_v2)
        swapped2 = over_x(swap_v2)
        swap_shift = over_row(swapped2)

        out = place_rows(0, place, rows_n, w, dh, cols, [own_v0, swapped0, *shifted0])
        out = place_rows(1, place, rows_n, w, dh, cols, [own_v1, swapped1, *shifted1], out)
        last = [own_v2, swapped2]
        for pair in zip(own_shift, swap_shift):
            last.extend(pair)
        return place_rows(2, place, rows_n, w, dh, cols, last, out)

    return on_device


def plain(lower_prev, inner_blocks, diag_inverse, known_rows, right_sides):
    highest = lax.Precision.HIGHEST
    row_count = lower_prev.shape[1]
    row_index = lax.axis_index("row")
    earlier_map = [[], [(0, 0)], [(0, 1), (1, 2)]]
    solved = []
    for section in range(3):
        update = jnp.dot(lower_prev[section], known_rows, precision=highest, preferred_element_type=F32)
        for earlier, which in earlier_map[section]:
            update = update + jnp.dot(
                inner_blocks[which], solved[earlier], precision=highest, preferred_element_type=F32
            )
        reduced = right_sides[section] - lax.psum(update, "depth")
        columns = lax.dynamic_slice_in_dim(diag_inverse[section], row_index * row_count, row_count, 1)
        partial_sum = jnp.dot(columns, reduced, precision=highest, preferred_element_type=F32)
        solved.append(lax.psum(partial_sum, "row"))
    return jnp.stack(solved)


def solution(mesh):
    placed = (
        P(None, "row", "depth"),
        P(None, "row", "depth"),
        P(None, "depth", None),
        P("depth", "col"),
        P(None, "row", "col"),
    )

    def run(*args):
        cols = args[3].shape[1] // mesh.shape["col"]
        tiles = cols % (2 * 128 * mesh.shape["row"]) == 0 and args[0].shape[1] % (256 * mesh.shape["row"]) == 0
        fits = mesh.shape["depth"] == 4 and mesh.shape["row"] % 2 == 0 and mesh.shape["col"] == 2
        body = make(mesh) if tiles and fits else plain
        return jax.shard_map(
            body, mesh=mesh, in_specs=placed, out_specs=P(None, "depth", "col"), check_vma=False
        )(*args)

    return run
```

```python
import functools

import jax
import jax.numpy as jnp
from jax import lax
from jax.experimental import pallas as pl
from jax.experimental.pallas import tpu as pltpu
from jax.sharding import PartitionSpec as P


F32 = jnp.float32
BF16 = jnp.bfloat16
SMEM = pl.BlockSpec(memory_space=pltpu.SMEM)
VMEM = pl.BlockSpec(memory_space=pltpu.VMEM)


def split(v):
    high = v.astype(BF16)
    return high, (v - high.astype(F32)).astype(BF16)


def mul(a, b):
    return jnp.dot(a, b, preferred_element_type=F32)


def mul3(a, b_high, b_both):
    a_high, a_low = split(a)
    n = b_high.shape[1]
    wide = mul(a_high, b_both)
    return wide[:, :n] + wide[:, n:] + mul(a_low, b_high)


def limit(mib):
    return pltpu.CompilerParams(vmem_limit_bytes=mib << 20)


def cost(flops, nbytes):
    return pl.CostEstimate(flops=flops, bytes_accessed=nbytes, transcendentals=0)


def prev_kernel(h, w, s_ref, a_ref, k_ref, *refs):
    outs, high_ref, low_ref = refs[:4], refs[4], refs[5]
    j = pl.program_id(0)
    y = s_ref[1]

    @pl.when(j == 0)
    def _():
        for rel in range(2):
            side = y if rel == 0 else 1 - y
            high, low = split(a_ref[pl.ds(pl.multiple_of(side * h, h), h), :])
            high_ref[rel * h : (rel + 1) * h, :] = high
            low_ref[rel * h : (rel + 1) * h, :] = low

    k_high, k_low = split(k_ref[...])
    part = mul(high_ref[...], k_high) + mul(high_ref[...], k_low) + mul(low_ref[...], k_high)
    per = k_ref.shape[1] // w
    for rel in range(4):

        @pl.when(j // 2 == rel % 2)
        def _():
            for n in range(per):
                outs[rel][(j % 2) * per + n] = part[
                    (rel // 2) * h : (rel // 2 + 1) * h, n * w : (n + 1) * w
                ]


def prev_product(place, lower_prev, known_rows, k, rows_n, h, w):
    rl, inner = lower_prev.shape[1:]
    cols = known_rows.shape[1]
    return pl.pallas_call(
        functools.partial(prev_kernel, h, w),
        grid_spec=pltpu.PrefetchScalarGridSpec(
            num_scalar_prefetch=1,
            grid=(4,),
            in_specs=[
                pl.BlockSpec((None, rl, inner), lambda j, s: (k, 0, 0)),
                pl.BlockSpec((inner, cols // 4), lambda j, s: (0, (s[0] ^ (j // 2)) * 2 + j % 2)),
            ],
            out_specs=[pl.BlockSpec((rows_n, h, w), lambda j, s: (0, 0, 0))] * 4,
            scratch_shapes=[pltpu.VMEM((rl, inner), BF16)] * 2,
        ),
        out_shape=[jax.ShapeDtypeStruct((rows_n, h, w), F32)] * 4,
        cost_estimate=cost(2 * rl * inner * cols * 3, 4 * (rl * inner + inner * cols + rl * cols)),
        compiler_params=limit(14),
    )(place, lower_prev, known_rows)


def sum_kernel(w, s_ref, p0, p1, p2, p3, b_ref, *outs):
    for i, o_ref in enumerate(outs):
        to = s_ref[2] ^ i
        total = (p0[to] + p1[to]) + (p2[to] + p3[to])
        o_ref[...] = b_ref[:, pl.ds(pl.multiple_of(to * w, w), w)] - total


def sum_parts(place, parts, right_sides, k):
    rows_n, h, w = parts[0].shape
    return pl.pallas_call(
        functools.partial(sum_kernel, w),
        grid_spec=pltpu.PrefetchScalarGridSpec(
            num_scalar_prefetch=1,
            grid=(1,),
            in_specs=[VMEM] * 4 + [pl.BlockSpec((None, h, rows_n * w), lambda i, s: (k, s[1], s[0]))],
            out_specs=[VMEM] * rows_n,
        ),
        out_shape=[jax.ShapeDtypeStruct((h, w), F32)] * rows_n,
        cost_estimate=cost(5 * rows_n * h * w, 24 * rows_n * h * w),
        compiler_params=limit(5),
    )(place, *parts, right_sides)


def step_kernel(k, rows_n, h, w, dh, s_ref, *refs):
    refs = list(refs)
    y, z, core = s_ref[1], s_ref[2], s_ref[3]
    value_ref = refs.pop()
    both_ref = refs.pop()
    first_ref = refs.pop() if k == 1 else None
    a_ref, b_ref = refs.pop(0), refs.pop(0)
    if k == 0:
        for i in range(rows_n):
            for at, src in ((y, a_ref), (1 - y, b_ref)):
                high, low = split(src[i])
                value_ref[z ^ i, at, :, :w] = high
                value_ref[z ^ i, at, :, w:] = low
    else:
        mine_ref, theirs_ref = refs.pop(0), refs.pop(0)
        for i in range(rows_n):
            for at in range(2):
                total = jnp.where(y == at, mine_ref[z ^ i], theirs_ref[z ^ i]) - (
                    a_ref[i, at] + b_ref[i, at]
                )
                high, low = split(total)
                value_ref[i, at, :, :w] = high
                value_ref[i, at, :, w:] = low
    reduced = value_ref[...].reshape(rows_n * 2 * h, 2 * w)
    d_ref, near_ref, far_ref = refs.pop(0), refs.pop(0), refs.pop(0)
    blocks = (
        d_ref[pl.ds(pl.multiple_of(core * dh, dh), dh), :],
        near_ref[...],
        d_ref[pl.ds(pl.multiple_of((1 - core) * dh, dh), dh), :],
        far_ref[...],
    )
    own_out, swap_out = (refs[-3], refs[-2]) if k < 2 else (refs[-2], refs[-1])
    for n, block in enumerate(blocks):
        value = mul3(block, reduced[:, :w], reduced)
        (own_out, swap_out)[n % 2][n // 2] = value
        if k < 2:
            high, low = split(value)
            both_ref[n * dh : (n + 1) * dh, :w] = high
            both_ref[n * dh : (n + 1) * dh, w:] = low
    if k == 2:
        return
    u_ref = refs[-1]
    if k == 0:
        pack_ref, other_ref = refs[0], refs[1]
        for i in range(rows_n):
            row = jnp.concatenate(
                [pack_ref[i, 0], pack_ref[i, 1], other_ref[i, 0], other_ref[i, 1]], 1
            )
            u = mul3(row, both_ref[:, :w], both_ref[...])
            at = z ^ i
            u_ref[at, 0] = u[:h]
            u_ref[at, 1] = u[h:]
    else:
        first_own, first_swap = refs[0], refs[1]
        mine, near, rest, far = refs[2:6]
        for n, ref in enumerate((first_own, first_swap) * 2):
            high, low = split(ref[n // 2])
            first_ref[n * dh : (n + 1) * dh, :w] = high
            first_ref[n * dh : (n + 1) * dh, w:] = low
        for i in range(rows_n):
            at = z ^ i
            total = None
            for block, values in ((0, first_ref), (1, both_ref)):
                row = jnp.concatenate([m[i, block] for m in (mine, near, rest, far)], 1)
                u = mul3(row, values[:, :w], values[...])
                total = u if total is None else total + u
            u_ref[at, 0] = total[:h]
            u_ref[at, 1] = total[h:]


def run_step(k, place, rows_n, h, w, dh, ins, diag, near, far, near_at, weights):
    nb = rows_n * 2 * h
    out = [jax.ShapeDtypeStruct((2, dh, w), F32)] * 2
    if k < 2:
        out.append(jax.ShapeDtypeStruct((rows_n, 2, h, w), F32))
    whole = pl.BlockSpec((None,) + diag.shape[1:], lambda i: (k, 0, 0))
    part = pl.BlockSpec((None,) + near.shape[1:], lambda i: (near_at, 0, 0))
    return pl.pallas_call(
        functools.partial(step_kernel, k, rows_n, h, w, dh),
        grid=(1,),
        in_specs=[SMEM] + [VMEM] * len(ins) + [whole, part, part] + [VMEM] * len(weights),
        out_specs=[VMEM] * len(out),
        out_shape=out,
        scratch_shapes=[pltpu.VMEM((4 * dh, 2 * w), BF16)] * (2 if k == 1 else 1)
        + [pltpu.VMEM((rows_n, 2, h, 2 * w), BF16)],
        cost_estimate=cost(12 * nb * 4 * dh * w, 8 * nb * 4 * dh),
        compiler_params=limit(16),
    )(place, *ins, diag, near, far, *weights)


def place_kernel(rows_n, w, dh, split_pairs, s_ref, *refs):
    x, z, core = s_ref[0], s_ref[2], s_ref[3]
    o_ref = refs[-1]
    pieces = [refs[:2]]
    for i in range(1, rows_n):
        pieces.append(refs[2 * i : 2 * i + 2] if split_pairs else refs[i + 1])
    for i in range(rows_n):
        member = z ^ i
        for rel in range(2):
            side = x if rel == 0 else 1 - x
            col = pl.multiple_of((side * rows_n + member) * w, w)
            for s in range(2):
                half = core if s == 0 else 1 - core
                row = pl.multiple_of(half * dh, dh)
                o_ref[pl.ds(row, dh), pl.ds(col, w)] = pieces[i][rel][s]


def place_rows(k, place, rows_n, w, dh, cols, ins, target=None):
    split_pairs = len(ins) == 2 * rows_n
    specs = [SMEM] + [VMEM] * len(ins)
    alias = {}
    if target is not None:
        ins = [*ins, target]
        specs.append(pl.BlockSpec(memory_space=pl.ANY))
        alias = {len(ins): 0}
    return pl.pallas_call(
        functools.partial(place_kernel, rows_n, w, dh, split_pairs),
        grid=(1,),
        in_specs=specs,
        out_specs=pl.BlockSpec((None, 2 * dh, cols), lambda i: (k, 0, 0)),
        out_shape=jax.ShapeDtypeStruct((3, 2 * dh, cols), F32),
        input_output_aliases=alias,
        cost_estimate=cost(0, 16 * dh * cols),
        compiler_params=limit(6),
    )(place, *ins)


def make(mesh):
    rows_n = mesh.shape["row"]
    depth_n = mesh.shape["depth"]
    pairs = {
        "x": ("depth", [(d, d ^ 1) for d in range(depth_n)]),
        "y": ("depth", [(d, d ^ 2) for d in range(depth_n)]),
        "core": ("col", [(0, 1), (1, 0)]),
        "z1": ("row", [(j, j ^ 1) for j in range(rows_n)]),
        "z2": ("row", [(j, j ^ 2) for j in range(rows_n)]),
        "z3": ("row", [(j, j ^ 3) for j in range(rows_n)]),
        "diag": ("depth", [(d, d ^ 3) for d in range(depth_n)]),
    }

    def move(way, v):
        return lax.ppermute(v, *pairs[way])

    def over_row(v):
        far = move("z2", v)
        near = move("z1", v)
        return near, far, move("z1", far)

    def body(lower_prev, inner_blocks, diag_inverse, known_rows, right_sides):
        z = lax.axis_index("row")
        d = lax.axis_index("depth")
        core = lax.axis_index("col")
        place = jnp.stack([d % 2, d // 2, z, core]).astype(jnp.int32)
        h = lower_prev.shape[1] // 2
        cols = known_rows.shape[1]
        w = cols // (2 * rows_n)
        dh = diag_inverse.shape[1] // 2
        lw = inner_blocks.shape[2] // 2

        def d_mine(k):
            return lax.dynamic_slice(diag_inverse, (k, core * dh, 0), (1, dh, diag_inverse.shape[2]))

        def l_mine(lo, hi):
            return lax.dynamic_slice(
                inner_blocks, (lo, 0, core * lw), (hi - lo, inner_blocks.shape[1], lw)
            )

        def parts(k):
            keep, x_part, y_part, d_part = prev_product(place, lower_prev, known_rows, k, rows_n, h, w)
            return [keep, move("x", x_part), move("y", y_part), move("diag", d_part)]

        def rows_of(pieces):
            got = [pieces[0], move("z1", pieces[1]), move("z2", pieces[2]), move("z3", pieces[3])]
            return jnp.stack(got)

        def diag(k):
            near = move("x", d_mine(k))
            return near, move("core", near)

        first = l_mine(0, 1)[0]
        pair10 = jnp.stack([first, move("x", first)])
        pack10 = jnp.stack([pair10, *over_row(pair10)])
        other10 = move("core", pack10)
        later = l_mine(1, 3)
        pack2 = jnp.stack([later, *over_row(later)])
        near2 = move("x", pack2)
        mats2 = (pack2, near2, move("core", pack2), move("core", near2))

        near_d = [None] * 3
        far_d = [None] * 3
        for k in range(3):
            near_d[k], far_d[k] = diag(k)

        own, their = [], []
        for k in range(3):
            total = sum_parts(place, parts(k), right_sides, k)
            own.append(rows_of(total))
            their.append(move("y", own[k]))

        def step(k, ins, weights):
            return run_step(
                k, place, rows_n, h, w, dh, ins, diag_inverse,
                near_d[k], far_d[k], 0, weights,
            )

        def ship(own_v, swap_v):
            swapped = move("x", swap_v)
            both = jnp.stack([own_v, swapped])
            return [own_v, swapped, *over_row(both)]

        own_v, swap_v, u0 = step(0, [own[0], their[0]], [pack10, other10])
        v0 = move("y", u0)
        first_v = [own_v, swap_v]
        out0 = ship(own_v, swap_v)
        own_v, swap_v, u1 = step(1, [u0, v0, own[1], their[1]], [*first_v, *mats2])
        v1 = move("y", u1)
        out1 = ship(own_v, swap_v)
        own_v, swap_v = step(2, [u1, v1, own[2], their[2]], [])
        swapped = move("x", swap_v)
        out2 = [own_v, swapped]
        for pair in zip(over_row(own_v), over_row(swapped)):
            out2.extend(pair)

        out = None
        for k, ins in enumerate((out0, out1, out2)):
            out = place_rows(k, place, rows_n, w, dh, cols, ins, out)
        return out

    return body


def plain(lower_prev, inner_blocks, diag_inverse, known_rows, right_sides):
    highest = lax.Precision.HIGHEST
    row_count = lower_prev.shape[1]
    row_index = lax.axis_index("row")
    earlier_map = [[], [(0, 0)], [(0, 1), (1, 2)]]
    solved = []
    for section in range(3):
        update = jnp.dot(lower_prev[section], known_rows, precision=highest, preferred_element_type=F32)
        for earlier, which in earlier_map[section]:
            update = update + jnp.dot(
                inner_blocks[which], solved[earlier], precision=highest, preferred_element_type=F32
            )
        reduced = right_sides[section] - lax.psum(update, "depth")
        columns = lax.dynamic_slice_in_dim(diag_inverse[section], row_index * row_count, row_count, 1)
        partial_sum = jnp.dot(columns, reduced, precision=highest, preferred_element_type=F32)
        solved.append(lax.psum(partial_sum, "row"))
    return jnp.stack(solved)


def solution(mesh):
    placed = (
        P(None, "row", "depth"),
        P(None, "row", "depth"),
        P(None, "depth", None),
        P("depth", "col"),
        P(None, "row", "col"),
    )

    def run(*args):
        cols = args[3].shape[1] // mesh.shape["col"]
        tiles = cols % (2 * 128 * mesh.shape["row"]) == 0 and args[0].shape[1] % (256 * mesh.shape["row"]) == 0
        fits = mesh.shape["depth"] == 4 and mesh.shape["row"] == 4 and mesh.shape["col"] == 2
        body = make(mesh) if tiles and fits else plain
        return jax.shard_map(
            body, mesh=mesh, in_specs=placed, out_specs=P(None, "depth", "col"), check_vma=False
        )(*args)

    return run
```

```python
import functools

import jax
import jax.numpy as jnp
from jax import lax
from jax.experimental import pallas as pl
from jax.experimental.pallas import tpu as pltpu
from jax.sharding import PartitionSpec as P


F32 = jnp.float32
BF16 = jnp.bfloat16
SMEM = pl.BlockSpec(memory_space=pltpu.SMEM)
VMEM = pl.BlockSpec(memory_space=pltpu.VMEM)


def split(v):
    high = v.astype(BF16)
    return high, (v - high.astype(F32)).astype(BF16)


def mul(a, b):
    return jnp.dot(a, b, preferred_element_type=F32)


def mul3(a, b_high, b_both):
    a_high, a_low = split(a)
    n = b_high.shape[1]
    wide = mul(a_high, b_both)
    return wide[:, :n] + wide[:, n:] + mul(a_low, b_high)


def limit(mib):
    return pltpu.CompilerParams(vmem_limit_bytes=mib << 20)


def cost(flops, nbytes):
    return pl.CostEstimate(flops=flops, bytes_accessed=nbytes, transcendentals=0)


def prev_kernel(k, h, w, s_ref, a_ref, k_ref, *outs):
    x, y = s_ref[0], s_ref[1]
    wide = k_ref.shape[1] // 4
    high, low = [], []
    for rel in range(2):
        side = y if rel == 0 else 1 - y
        a_high, a_low = split(a_ref[k, pl.ds(pl.multiple_of(side * h, h), h), :])
        high.append(a_high)
        low.append(a_low)
    a_high, a_low = jnp.concatenate(high, 0), jnp.concatenate(low, 0)
    per = wide // w
    for j in range(4):
        at = pl.multiple_of(((x ^ (j // 2)) * 2 + j % 2) * wide, wide)
        k_high, k_low = split(k_ref[:, pl.ds(at, wide)])
        part = mul(a_high, k_high) + mul(a_high, k_low) + mul(a_low, k_high)
        for ry in range(2):
            for n in range(per):
                outs[ry][j // 2, (j % 2) * per + n] = part[ry * h : (ry + 1) * h, n * w : (n + 1) * w]


def prev_product(place, lower_prev, known_rows, k, rows_n, h, w):
    rl, inner = lower_prev.shape[1:]
    cols = known_rows.shape[1]
    return pl.pallas_call(
        functools.partial(prev_kernel, k, h, w),
        in_specs=[SMEM, VMEM, VMEM],
        out_specs=[VMEM] * 2,
        out_shape=[jax.ShapeDtypeStruct((2, rows_n, h, w), F32)] * 2,
        cost_estimate=cost(2 * rl * inner * cols * 3, 4 * (rl * inner + inner * cols + rl * cols)),
        compiler_params=limit(16),
    )(place, lower_prev, known_rows)


def pack_kernel(*refs):
    for n, piece in enumerate(refs[:-1]):
        refs[-1][n] = piece[...]


def pack(pieces):
    return pl.pallas_call(
        pack_kernel,
        in_specs=[VMEM] * len(pieces),
        out_specs=VMEM,
        out_shape=jax.ShapeDtypeStruct((len(pieces), *pieces[0].shape), F32),
        cost_estimate=cost(0, 8 * len(pieces) * pieces[0].size),
        compiler_params=limit(4),
    )(*pieces)


def add_kernel(keep_ref, got_ref, stay_ref, go_ref):
    go_ref[...] = keep_ref[1] + got_ref[1]
    stay_ref[...] = keep_ref[0] + got_ref[0]


def add_parts(keep, got):
    shape = jax.ShapeDtypeStruct(keep.shape[1:], F32)
    return pl.pallas_call(
        add_kernel,
        in_specs=[VMEM] * 2,
        out_specs=[VMEM] * 2,
        out_shape=[shape] * 2,
        cost_estimate=cost(keep.size, 12 * keep.size),
        compiler_params=limit(4),
    )(keep, got)


def sum_kernel(w, s_ref, *refs):
    parts, b_ref, outs = refs[:-5], refs[-5], refs[-4:]
    for i, o_ref in enumerate(outs):
        to = s_ref[2] ^ i
        terms = [p[to] for p in parts]
        while len(terms) > 1:
            terms = [terms[n] + terms[n + 1] for n in range(0, len(terms), 2)]
        o_ref[...] = b_ref[:, pl.ds(pl.multiple_of(to * w, w), w)] - terms[0]


def sum_parts(place, parts, right_sides, k):
    rows_n, h, w = parts[0].shape
    return pl.pallas_call(
        functools.partial(sum_kernel, w),
        grid_spec=pltpu.PrefetchScalarGridSpec(
            num_scalar_prefetch=1,
            grid=(1,),
            in_specs=[VMEM] * len(parts)
            + [pl.BlockSpec((None, h, rows_n * w), lambda i, s: (k, s[1], s[0]))],
            out_specs=[VMEM] * rows_n,
        ),
        out_shape=[jax.ShapeDtypeStruct((h, w), F32)] * rows_n,
        cost_estimate=cost(5 * rows_n * h * w, 24 * rows_n * h * w),
        compiler_params=limit(5),
    )(place, *parts, right_sides)


def step_kernel(k, rows_n, h, w, dh, s_ref, *refs):
    refs = list(refs)
    y, z, core = s_ref[1], s_ref[2], s_ref[3]
    value_ref = refs.pop()
    both_ref = refs.pop()
    first_ref = refs.pop() if k == 1 else None
    a_ref, b_ref = refs.pop(0), refs.pop(0)
    if k == 0:
        for i in range(rows_n):
            for at, src in ((y, a_ref), (1 - y, b_ref)):
                high, low = split(src[i])
                value_ref[z ^ i, at, :, :w] = high
                value_ref[z ^ i, at, :, w:] = low
    else:
        if k == 1:
            mine_ref, theirs_ref = refs.pop(0), refs.pop(0)
        for i in range(rows_n):
            for at in range(2):
                total = a_ref[i, at] + b_ref[i, at]
                if k == 1:
                    total = total - jnp.where(y == at, mine_ref[z ^ i], theirs_ref[z ^ i])
                high, low = split(-total)
                value_ref[i, at, :, :w] = high
                value_ref[i, at, :, w:] = low
    reduced = value_ref[...].reshape(rows_n * 2 * h, 2 * w)
    d_ref, near_ref, far_ref = refs.pop(0), refs.pop(0), refs.pop(0)
    blocks = (
        d_ref[pl.ds(pl.multiple_of(core * dh, dh), dh), :],
        near_ref[...],
        d_ref[pl.ds(pl.multiple_of((1 - core) * dh, dh), dh), :],
        far_ref[...],
    )
    own_out, swap_out = (refs[-3], refs[-2]) if k < 2 else (refs[-2], refs[-1])
    for n, block in enumerate(blocks):
        value = mul3(block, reduced[:, :w], reduced)
        (own_out, swap_out)[n % 2][n // 2] = value
        if k < 2:
            high, low = split(value)
            both_ref[n * dh : (n + 1) * dh, :w] = high
            both_ref[n * dh : (n + 1) * dh, w:] = low
    if k == 2:
        return
    u_ref = refs[-1]
    next_refs = [refs.pop(0) for _ in range(rows_n)] if k == 1 else None
    if k == 0:
        pack_ref, other_ref = refs[0], refs[1]
        for i in range(rows_n):
            row = jnp.concatenate(
                [pack_ref[i, 0], pack_ref[i, 1], other_ref[i, 0], other_ref[i, 1]], 1
            )
            u = mul3(row, both_ref[:, :w], both_ref[...])
            at = z ^ i
            u_ref[at, 0] = u[:h]
            u_ref[at, 1] = u[h:]
    else:
        first_own, first_swap = refs[0], refs[1]
        mine, near, rest, far = refs[2:6]
        for n, ref in enumerate((first_own, first_swap) * 2):
            high, low = split(ref[n // 2])
            first_ref[n * dh : (n + 1) * dh, :w] = high
            first_ref[n * dh : (n + 1) * dh, w:] = low
        for i in range(rows_n):
            at = z ^ i
            total = None
            for block, values in ((0, first_ref), (1, both_ref)):
                row = jnp.concatenate([m[i, block] for m in (mine, near, rest, far)], 1)
                u = mul3(row, values[:, :w], values[...])
                total = u if total is None else total + u
            for part in range(2):
                u_ref[at, part] = total[part * h : (part + 1) * h] - jnp.where(
                    y == part, next_refs[i][...], 0.0
                )


def run_step(k, place, rows_n, h, w, dh, ins, diag, near, far, near_at, weights):
    nb = rows_n * 2 * h
    out = [jax.ShapeDtypeStruct((2, dh, w), F32)] * 2
    if k < 2:
        out.append(jax.ShapeDtypeStruct((rows_n, 2, h, w), F32))
    whole = pl.BlockSpec((None,) + diag.shape[1:], lambda i: (k, 0, 0))
    part = pl.BlockSpec((None,) + near.shape[1:], lambda i: (near_at, 0, 0))
    return pl.pallas_call(
        functools.partial(step_kernel, k, rows_n, h, w, dh),
        grid=(1,),
        in_specs=[SMEM] + [VMEM] * len(ins) + [whole, part, part] + [VMEM] * len(weights),
        out_specs=[VMEM] * len(out),
        out_shape=out,
        scratch_shapes=[pltpu.VMEM((4 * dh, 2 * w), BF16)] * (2 if k == 1 else 1)
        + [pltpu.VMEM((rows_n, 2, h, 2 * w), BF16)],
        cost_estimate=cost(12 * nb * 4 * dh * w, 8 * nb * 4 * dh),
        compiler_params=limit(16),
    )(place, *ins, diag, near, far, *weights)


def place_kernel(rows_n, w, dh, split_pairs, s_ref, *refs):
    x, z, core = s_ref[0], s_ref[2], s_ref[3]
    o_ref = refs[-1]
    pieces = [refs[:2]]
    for i in range(1, rows_n):
        pieces.append(refs[2 * i : 2 * i + 2] if split_pairs else refs[i + 1])
    for i in range(rows_n):
        member = z ^ i
        for rel in range(2):
            side = x if rel == 0 else 1 - x
            col = pl.multiple_of((side * rows_n + member) * w, w)
            for s in range(2):
                half = core if s == 0 else 1 - core
                row = pl.multiple_of(half * dh, dh)
                o_ref[pl.ds(row, dh), pl.ds(col, w)] = pieces[i][rel][s]


def place_rows(k, place, rows_n, w, dh, cols, ins, target=None):
    split_pairs = len(ins) == 2 * rows_n
    specs = [SMEM] + [VMEM] * len(ins)
    alias = {}
    if target is not None:
        ins = [*ins, target]
        specs.append(pl.BlockSpec(memory_space=pl.ANY))
        alias = {len(ins): 0}
    return pl.pallas_call(
        functools.partial(place_kernel, rows_n, w, dh, split_pairs),
        grid=(1,),
        in_specs=specs,
        out_specs=pl.BlockSpec((None, 2 * dh, cols), lambda i: (k, 0, 0)),
        out_shape=jax.ShapeDtypeStruct((3, 2 * dh, cols), F32),
        input_output_aliases=alias,
        cost_estimate=cost(0, 16 * dh * cols),
        compiler_params=limit(6),
    )(place, *ins)


def make(mesh):
    rows_n = mesh.shape["row"]
    depth_n = mesh.shape["depth"]
    pairs = {
"x": ("depth", [(d, d ^ 1) for d in range(depth_n)]),
"y": ("depth", [(d, d ^ 2) for d in range(depth_n)]),
"core": ("col", [(0, 1), (1, 0)]),
"z1": ("row", [(j, j ^ 1) for j in range(rows_n)]),
"z2": ("row", [(j, j ^ 2) for j in range(rows_n)]),
"z3": ("row", [(j, j ^ 3) for j in range(rows_n)]),
    }

    def move(way, v):
        return lax.ppermute(v, *pairs[way])

    def over_row(v):
        far = move("z2", v)
        near = move("z1", v)
        return near, far, move("z1", far)

    def body(lower_prev, inner_blocks, diag_inverse, known_rows, right_sides):
        z = lax.axis_index("row")
        d = lax.axis_index("depth")
        core = lax.axis_index("col")
        place = jnp.stack([d % 2, d // 2, z, core]).astype(jnp.int32)
        h = lower_prev.shape[1] // 2
        cols = known_rows.shape[1]
        w = cols // (2 * rows_n)
        dh = diag_inverse.shape[1] // 2
        lw = inner_blocks.shape[2] // 2

        def d_mine(k):
            return lax.dynamic_slice(diag_inverse, (k, core * dh, 0), (1, dh, diag_inverse.shape[2]))

        def l_mine(lo, hi):
            return lax.dynamic_slice(
                inner_blocks, (lo, 0, core * lw), (hi - lo, inner_blocks.shape[1], lw)
            )

        def parts(k):
            keep, send = prev_product(place, lower_prev, known_rows, k, rows_n, h, w)
            got = move("y", send)
            stay, go = add_parts(keep, got)
            return [stay, move("x", go)]

        def rows_of(pieces):
            got = [pieces[0], move("z1", pieces[1]), move("z2", pieces[2]), move("z3", pieces[3])]
            return got

        def diag(k):
            near = move("x", d_mine(k))
            return near, move("core", near)

        first = l_mine(0, 1)[0]
        pair10 = pack([first, move("x", first)])
        got10 = over_row(pair10)
        pack10 = pack([pair10, *got10])
        other10 = move("core", pack10)
        later = l_mine(1, 3)
        got2 = over_row(later)
        pack2 = pack([later, *got2])
        near2 = move("x", pack2)
        mats2 = (pack2, near2, move("core", pack2), move("core", near2))

        near_d = [None] * 3
        far_d = [None] * 3
        for k in range(3):
            near_d[k], far_d[k] = diag(k)

        own = []
        for k in range(3):
            total = sum_parts(place, parts(k), right_sides, k)
            own.append(rows_of(total))
        mine = [pack(own[k]) for k in range(2)]
        theirs = [move("y", mine[k]) for k in range(2)]

        def step(k, ins, weights):
            return run_step(
                k, place, rows_n, h, w, dh, ins, diag_inverse,
                near_d[k], far_d[k], 0, weights,
            )

        def ship(own_v, swap_v):
            swapped = move("x", swap_v)
            both = pack([own_v, swapped])
            return [own_v, swapped, *over_row(both)]

        own_v, swap_v, u0 = step(0, [mine[0], theirs[0]], [pack10, other10])
        v0 = move("y", u0)
        first_v = [own_v, swap_v]
        out0 = ship(own_v, swap_v)
        own_v, swap_v, u1 = step(1, [u0, v0, mine[1], theirs[1]], [*own[2], *first_v, *mats2])
        v1 = move("y", u1)
        out1 = ship(own_v, swap_v)
        own_v, swap_v = step(2, [u1, v1], [])
        swapped = move("x", swap_v)
        out2 = [own_v, swapped]
        for pair in zip(over_row(own_v), over_row(swapped)):
            out2.extend(pair)

        out = None
        for k, ins in enumerate((out0, out1, out2)):
            out = place_rows(k, place, rows_n, w, dh, cols, ins, out)
        return out

    return body


def plain(lower_prev, inner_blocks, diag_inverse, known_rows, right_sides):
    highest = lax.Precision.HIGHEST
    row_count = lower_prev.shape[1]
    row_index = lax.axis_index("row")
    earlier_map = [[], [(0, 0)], [(0, 1), (1, 2)]]
    solved = []
    for section in range(3):
        update = jnp.dot(lower_prev[section], known_rows, precision=highest, preferred_element_type=F32)
        for earlier, which in earlier_map[section]:
            update = update + jnp.dot(
                inner_blocks[which], solved[earlier], precision=highest, preferred_element_type=F32
            )
        reduced = right_sides[section] - lax.psum(update, "depth")
        columns = lax.dynamic_slice_in_dim(diag_inverse[section], row_index * row_count, row_count, 1)
        partial_sum = jnp.dot(columns, reduced, precision=highest, preferred_element_type=F32)
        solved.append(lax.psum(partial_sum, "row"))
    return jnp.stack(solved)


def solution(mesh):
    placed = (
        P(None, "row", "depth"),
        P(None, "row", "depth"),
        P(None, "depth", None),
        P("depth", "col"),
        P(None, "row", "col"),
    )

    def run(*args):
        cols = args[3].shape[1] // mesh.shape["col"]
        tiles = cols % (2 * 128 * mesh.shape["row"]) == 0 and args[0].shape[1] % (256 * mesh.shape["row"]) == 0
        fits = mesh.shape["depth"] == 4 and mesh.shape["row"] == 4 and mesh.shape["col"] == 2
        body = make(mesh) if tiles and fits else plain
        return jax.shard_map(
            body, mesh=mesh, in_specs=placed, out_specs=P(None, "depth", "col"), check_vma=False
        )(*args)

    return run
```

```python
import functools

import jax
import jax.numpy as jnp
from jax import lax
from jax.experimental import pallas as pl
from jax.experimental.pallas import tpu as pltpu
from jax.sharding import PartitionSpec as P


F32 = jnp.float32
BF16 = jnp.bfloat16
SMEM = pl.BlockSpec(memory_space=pltpu.SMEM)
VMEM = pl.BlockSpec(memory_space=pltpu.VMEM)


def split(v):
    high = v.astype(BF16)
    return high, (v - high.astype(F32)).astype(BF16)


def mul(a, b):
    return jnp.dot(a, b, preferred_element_type=F32)


def mul3(a, b_high, b_both):
    a_high, a_low = split(a)
    n = b_high.shape[1]
    wide = mul(a_high, b_both)
    return wide[:, :n] + wide[:, n:] + mul(a_low, b_high)


def limit(mib):
    return pltpu.CompilerParams(vmem_limit_bytes=mib << 20)


def cost(flops, nbytes):
    return pl.CostEstimate(flops=flops, bytes_accessed=nbytes, transcendentals=0)


def prev_kernel(k, h, w, s_ref, a_ref, k_ref, *outs):
    x, y = s_ref[0], s_ref[1]
    wide = k_ref.shape[1] // 4
    high, low = [], []
    for rel in range(2):
        side = y if rel == 0 else 1 - y
        a_high, a_low = split(a_ref[k, pl.ds(pl.multiple_of(side * h, h), h), :])
        high.append(a_high)
        low.append(a_low)
    a_high, a_low = jnp.concatenate(high, 0), jnp.concatenate(low, 0)
    per = wide // w
    for j in range(4):
        at = pl.multiple_of(((x ^ (j // 2)) * 2 + j % 2) * wide, wide)
        k_high, k_low = split(k_ref[:, pl.ds(at, wide)])
        part = mul(a_high, k_high) + mul(a_high, k_low) + mul(a_low, k_high)
        for ry in range(2):
            for n in range(per):
                outs[ry][j // 2, (j % 2) * per + n] = part[ry * h : (ry + 1) * h, n * w : (n + 1) * w]


def prev_product(place, lower_prev, known_rows, k, rows_n, h, w):
    rl, inner = lower_prev.shape[1:]
    cols = known_rows.shape[1]
    return pl.pallas_call(
        functools.partial(prev_kernel, k, h, w),
        in_specs=[SMEM, VMEM, VMEM],
        out_specs=[VMEM] * 2,
        out_shape=[jax.ShapeDtypeStruct((2, rows_n, h, w), F32)] * 2,
        cost_estimate=cost(2 * rl * inner * cols * 3, 4 * (rl * inner + inner * cols + rl * cols)),
        compiler_params=limit(16),
    )(place, lower_prev, known_rows)


def pack_kernel(*refs):
    for n, piece in enumerate(refs[:-1]):
        refs[-1][n] = piece[...]


def pack(pieces):
    return pl.pallas_call(
        pack_kernel,
        in_specs=[VMEM] * len(pieces),
        out_specs=VMEM,
        out_shape=jax.ShapeDtypeStruct((len(pieces), *pieces[0].shape), F32),
        cost_estimate=cost(0, 8 * len(pieces) * pieces[0].size),
        compiler_params=limit(4),
    )(*pieces)


def add_kernel(keep_ref, got_ref, stay_ref, go_ref):
    go_ref[...] = keep_ref[1] + got_ref[1]
    stay_ref[...] = keep_ref[0] + got_ref[0]


def add_parts(keep, got):
    shape = jax.ShapeDtypeStruct(keep.shape[1:], F32)
    return pl.pallas_call(
        add_kernel,
        in_specs=[VMEM] * 2,
        out_specs=[VMEM] * 2,
        out_shape=[shape] * 2,
        cost_estimate=cost(keep.size, 12 * keep.size),
        compiler_params=limit(4),
    )(keep, got)


def sum_kernel(w, s_ref, *refs):
    parts, b_ref, outs = refs[:-5], refs[-5], refs[-4:]
    for i, o_ref in enumerate(outs):
        to = s_ref[2] ^ i
        terms = [p[to] for p in parts]
        while len(terms) > 1:
            terms = [terms[n] + terms[n + 1] for n in range(0, len(terms), 2)]
        o_ref[...] = b_ref[:, pl.ds(pl.multiple_of(to * w, w), w)] - terms[0]


def sum_parts(place, parts, right_sides, k):
    rows_n, h, w = parts[0].shape
    return pl.pallas_call(
        functools.partial(sum_kernel, w),
        grid_spec=pltpu.PrefetchScalarGridSpec(
            num_scalar_prefetch=1,
            grid=(1,),
            in_specs=[VMEM] * len(parts)
            + [pl.BlockSpec((None, h, rows_n * w), lambda i, s: (k, s[1], s[0]))],
            out_specs=[VMEM] * rows_n,
        ),
        out_shape=[jax.ShapeDtypeStruct((h, w), F32)] * rows_n,
        cost_estimate=cost(5 * rows_n * h * w, 24 * rows_n * h * w),
        compiler_params=limit(5),
    )(place, *parts, right_sides)


def step_kernel(k, rows_n, h, w, dh, s_ref, *refs):
    refs = list(refs)
    y, z, core = s_ref[1], s_ref[2], s_ref[3]
    value_ref = refs.pop()
    both_ref = refs.pop()
    first_ref = refs.pop() if k == 1 else None
    a_ref, b_ref = refs.pop(0), refs.pop(0)
    if k == 0:
        for i in range(rows_n):
            for at, src in ((y, a_ref), (1 - y, b_ref)):
                high, low = split(src[i])
                value_ref[z ^ i, at, :, :w] = high
                value_ref[z ^ i, at, :, w:] = low
    else:
        if k == 1:
            mine_ref, theirs_ref = refs.pop(0), refs.pop(0)
        for i in range(rows_n):
            for at in range(2):
                total = a_ref[i, at] + b_ref[i, at]
                if k == 1:
                    total = total - jnp.where(y == at, mine_ref[z ^ i], theirs_ref[z ^ i])
                high, low = split(-total)
                value_ref[i, at, :, :w] = high
                value_ref[i, at, :, w:] = low
    reduced = value_ref[...].reshape(rows_n * 2 * h, 2 * w)
    d_ref, near_ref, far_ref = refs.pop(0), refs.pop(0), refs.pop(0)
    blocks = (
        d_ref[pl.ds(pl.multiple_of(core * dh, dh), dh), :],
        near_ref[...],
        d_ref[pl.ds(pl.multiple_of((1 - core) * dh, dh), dh), :],
        far_ref[...],
    )
    own_out, swap_out = (refs[-3], refs[-2]) if k < 2 else (refs[-2], refs[-1])
    for n, block in enumerate(blocks):
        value = mul3(block, reduced[:, :w], reduced)
        (own_out, swap_out)[n % 2][n // 2] = value
        if k < 2:
            high, low = split(value)
            both_ref[n * dh : (n + 1) * dh, :w] = high
            both_ref[n * dh : (n + 1) * dh, w:] = low
    if k == 2:
        return
    u_ref = refs[-1]
    next_refs = [refs.pop(0) for _ in range(rows_n)] if k == 1 else None
    if k == 0:
        pack_ref, other_ref = refs[0], refs[1]
        for i in range(rows_n):
            row = jnp.concatenate(
                [pack_ref[i, 0], pack_ref[i, 1], other_ref[i, 0], other_ref[i, 1]], 1
            )
            u = mul3(row, both_ref[:, :w], both_ref[...])
            at = z ^ i
            u_ref[at, 0] = u[:h]
            u_ref[at, 1] = u[h:]
    else:
        first_own, first_swap = refs[0], refs[1]
        mine, near, rest, far = refs[2:6]
        for n, ref in enumerate((first_own, first_swap) * 2):
            high, low = split(ref[n // 2])
            first_ref[n * dh : (n + 1) * dh, :w] = high
            first_ref[n * dh : (n + 1) * dh, w:] = low
        for i in range(rows_n):
            at = z ^ i
            total = None
            for block, values in ((0, first_ref), (1, both_ref)):
                row = jnp.concatenate([m[i, block] for m in (mine, near, rest, far)], 1)
                u = mul3(row, values[:, :w], values[...])
                total = u if total is None else total + u
            for part in range(2):
                u_ref[at, part] = total[part * h : (part + 1) * h] - jnp.where(
                    y == part, next_refs[i][...], 0.0
                )


def run_step(k, place, rows_n, h, w, dh, ins, diag, near, far, near_at, weights):
    nb = rows_n * 2 * h
    out = [jax.ShapeDtypeStruct((2, dh, w), F32)] * 2
    if k < 2:
        out.append(jax.ShapeDtypeStruct((rows_n, 2, h, w), F32))
    whole = pl.BlockSpec((None,) + diag.shape[1:], lambda i: (k, 0, 0))
    part = pl.BlockSpec((None,) + near.shape[1:], lambda i: (near_at, 0, 0))
    return pl.pallas_call(
        functools.partial(step_kernel, k, rows_n, h, w, dh),
        grid=(1,),
        in_specs=[SMEM] + [VMEM] * len(ins) + [whole, part, part] + [VMEM] * len(weights),
        out_specs=[VMEM] * len(out),
        out_shape=out,
        scratch_shapes=[pltpu.VMEM((4 * dh, 2 * w), BF16)] * (2 if k == 1 else 1)
        + [pltpu.VMEM((rows_n, 2, h, 2 * w), BF16)],
        cost_estimate=cost(12 * nb * 4 * dh * w, 8 * nb * 4 * dh),
        compiler_params=limit(16),
    )(place, *ins, diag, near, far, *weights)


def place_kernel(rows_n, w, dh, split_pairs, s_ref, *refs):
    x, z, core = s_ref[0], s_ref[2], s_ref[3]
    o_ref = refs[-1]
    pieces = [refs[:2]]
    for i in range(1, rows_n):
        pieces.append(refs[2 * i : 2 * i + 2] if split_pairs else refs[i + 1])
    if split_pairs:
        pieces[-1] = pieces[-1][:1]
    for i in range(rows_n):
        member = z ^ i
        for rel in range(2 if i < rows_n - 1 or not split_pairs else 1):
            side = x if rel == 0 else 1 - x
            col = pl.multiple_of((side * rows_n + member) * w, w)
            for s in range(2):
                half = core if s == 0 else 1 - core
                row = pl.multiple_of(half * dh, dh)
                o_ref[pl.ds(row, dh), pl.ds(col, w)] = pieces[i][rel][s]


def place_rows(k, place, rows_n, w, dh, cols, ins, target=None):
    split_pairs = len(ins) > rows_n + 1
    specs = [SMEM] + [VMEM] * len(ins)
    alias = {}
    if target is not None:
        ins = [*ins, target]
        specs.append(pl.BlockSpec(memory_space=pl.ANY))
        alias = {len(ins): 0}
    return pl.pallas_call(
        functools.partial(place_kernel, rows_n, w, dh, split_pairs),
        grid=(1,),
        in_specs=specs,
        out_specs=pl.BlockSpec((None, 2 * dh, cols), lambda i: (k, 0, 0)),
        out_shape=jax.ShapeDtypeStruct((3, 2 * dh, cols), F32),
        input_output_aliases=alias,
        cost_estimate=cost(0, 16 * dh * cols),
        compiler_params=limit(6),
    )(place, *ins)


def last_kernel(s_ref, piece_ref, _, o_ref):
    dh = piece_ref.shape[1]
    for n in range(2):
        half = s_ref[3] if n == 0 else 1 - s_ref[3]
        o_ref[pl.ds(pl.multiple_of(half * dh, dh), dh), :] = piece_ref[n]


def place_last(k, place, rows_n, piece, target):
    _, dh, w = piece.shape
    return pl.pallas_call(
        last_kernel,
        grid_spec=pltpu.PrefetchScalarGridSpec(
            num_scalar_prefetch=1,
            grid=(1,),
            in_specs=[VMEM, pl.BlockSpec(memory_space=pl.ANY)],
            out_specs=pl.BlockSpec(
                (None, 2 * dh, w), lambda i, s: (k, 0, (1 - s[0]) * rows_n + (s[2] ^ (rows_n - 1)))
            ),
        ),
        out_shape=jax.ShapeDtypeStruct(target.shape, F32),
        input_output_aliases={2: 0},
        cost_estimate=cost(0, 8 * piece.size),
        compiler_params=limit(2),
        name="last",
    )(place, piece, target)


def make(mesh):
    rows_n = mesh.shape["row"]
    depth_n = mesh.shape["depth"]
    pairs = {
"x": ("depth", [(d, d ^ 1) for d in range(depth_n)]),
"y": ("depth", [(d, d ^ 2) for d in range(depth_n)]),
"core": ("col", [(0, 1), (1, 0)]),
"z1": ("row", [(j, j ^ 1) for j in range(rows_n)]),
"z2": ("row", [(j, j ^ 2) for j in range(rows_n)]),
"z3": ("row", [(j, j ^ 3) for j in range(rows_n)]),
    }

    def move(way, v):
        return lax.ppermute(v, *pairs[way])

    def over_row(v):
        far = move("z2", v)
        near = move("z1", v)
        return near, far, move("z1", far)

    def body(lower_prev, inner_blocks, diag_inverse, known_rows, right_sides):
        z = lax.axis_index("row")
        d = lax.axis_index("depth")
        core = lax.axis_index("col")
        place = jnp.stack([d % 2, d // 2, z, core]).astype(jnp.int32)
        h = lower_prev.shape[1] // 2
        cols = known_rows.shape[1]
        w = cols // (2 * rows_n)
        dh = diag_inverse.shape[1] // 2
        lw = inner_blocks.shape[2] // 2

        def d_mine(k):
            return lax.dynamic_slice(diag_inverse, (k, core * dh, 0), (1, dh, diag_inverse.shape[2]))

        def l_mine(lo, hi):
            return lax.dynamic_slice(
                inner_blocks, (lo, 0, core * lw), (hi - lo, inner_blocks.shape[1], lw)
            )

        def parts(k):
            keep, send = prev_product(place, lower_prev, known_rows, k, rows_n, h, w)
            got = move("y", send)
            stay, go = add_parts(keep, got)
            return [stay, move("x", go)]

        def rows_of(pieces):
            got = [pieces[0], move("z1", pieces[1]), move("z2", pieces[2]), move("z3", pieces[3])]
            return got

        def diag(k):
            near = move("x", d_mine(k))
            return near, move("core", near)

        first = l_mine(0, 1)[0]
        pair10 = pack([first, move("x", first)])
        got10 = over_row(pair10)
        pack10 = pack([pair10, *got10])
        other10 = move("core", pack10)
        later = l_mine(1, 3)
        got2 = over_row(later)
        pack2 = pack([later, *got2])
        near2 = move("x", pack2)
        mats2 = (pack2, near2, move("core", pack2), move("core", near2))

        near_d = [None] * 3
        far_d = [None] * 3
        for k in range(3):
            near_d[k], far_d[k] = diag(k)

        own = []
        for k in range(3):
            total = sum_parts(place, parts(k), right_sides, k)
            own.append(rows_of(total))
        mine = [pack(own[k]) for k in range(2)]
        theirs = [move("y", mine[k]) for k in range(2)]

        def step(k, ins, weights):
            return run_step(
                k, place, rows_n, h, w, dh, ins, diag_inverse,
                near_d[k], far_d[k], 0, weights,
            )

        def ship(own_v, swap_v):
            swapped = move("x", swap_v)
            both = pack([own_v, swapped])
            return [own_v, swapped, *over_row(both)]

        own_v, swap_v, u0 = step(0, [mine[0], theirs[0]], [pack10, other10])
        v0 = move("y", u0)
        first_v = [own_v, swap_v]
        out0 = ship(own_v, swap_v)
        own_v, swap_v, u1 = step(1, [u0, v0, mine[1], theirs[1]], [*own[2], *first_v, *mats2])
        v1 = move("y", u1)
        out1 = ship(own_v, swap_v)
        own_v, swap_v = step(2, [u1, v1], [])
        swapped = move("x", swap_v)
        out2 = [own_v, swapped]
        for pair in zip(over_row(own_v), over_row(swapped)):
            out2.extend(pair)

        out = None
        for k, ins in enumerate((out0, out1, out2)):
            out = place_rows(k, place, rows_n, w, dh, cols, ins[: 2 * rows_n - 1], out)
        return place_last(2, place, rows_n, out2[-1], out)

    return body


def plain(lower_prev, inner_blocks, diag_inverse, known_rows, right_sides):
    highest = lax.Precision.HIGHEST
    row_count = lower_prev.shape[1]
    row_index = lax.axis_index("row")
    earlier_map = [[], [(0, 0)], [(0, 1), (1, 2)]]
    solved = []
    for section in range(3):
        update = jnp.dot(lower_prev[section], known_rows, precision=highest, preferred_element_type=F32)
        for earlier, which in earlier_map[section]:
            update = update + jnp.dot(
                inner_blocks[which], solved[earlier], precision=highest, preferred_element_type=F32
            )
        reduced = right_sides[section] - lax.psum(update, "depth")
        columns = lax.dynamic_slice_in_dim(diag_inverse[section], row_index * row_count, row_count, 1)
        partial_sum = jnp.dot(columns, reduced, precision=highest, preferred_element_type=F32)
        solved.append(lax.psum(partial_sum, "row"))
    return jnp.stack(solved)


def solution(mesh):
    placed = (
        P(None, "row", "depth"),
        P(None, "row", "depth"),
        P(None, "depth", None),
        P("depth", "col"),
        P(None, "row", "col"),
    )

    def run(*args):
        cols = args[3].shape[1] // mesh.shape["col"]
        tiles = cols % (2 * 128 * mesh.shape["row"]) == 0 and args[0].shape[1] % (256 * mesh.shape["row"]) == 0
        fits = mesh.shape["depth"] == 4 and mesh.shape["row"] == 4 and mesh.shape["col"] == 2
        body = make(mesh) if tiles and fits else plain
        return jax.shard_map(
            body, mesh=mesh, in_specs=placed, out_specs=P(None, "depth", "col"), check_vma=False
        )(*args)

    return run
```
